32 devices in a mesh: wa: 4 (over z), vert: 8 (over y, x, core).
Axes of the slice: x: 2, y: 2, z: 4, core: 2. Of those that a mesh axis runs over, the one named last changes fastest.
Arguments:
- hidden_in: bfloat16 [384, 8192], P(None, 'wa')
- gate_levels: bfloat16 [8192, 28672], P('wa', 'vert'), may hold values from -127 to 127, as said below
- up_levels: bfloat16 [8192, 28672], P('wa', 'vert'), may hold values from -127 to 127, as said below
- gate_scale: float32 [28672], P('vert'), as said below
- up_scale: float32 [28672], P('vert'), as said below
- down_levels: bfloat16 [28672, 8192], P('vert', 'wa'), may hold values from -127 to 127, as said below
- down_scale: float32 [8192], P('wa'), as said below
- norm_gain: float32 [8192], P('wa'), may hold values from 0.5 to 1.5
- head_weight: bfloat16 [8192, 16000], P('wa', 'vert')
- reward_states: bfloat16 [4, 384, 4096], P('wa', None, 'vert'), may hold values from -6 to 6
- reward_gain: float32 [4, 4096], P('wa'), may hold values from 0.5 to 1.5
- reward_heads: bfloat16 [4, 4096, 16000], P('wa', None, 'vert')
- preference: int32 [384, 4], P(None, 'wa'), may hold values from 0 to 16
- token_ids: int32 [384], P('wa'), may hold values from 0 to 15999
Outputs:
- log_probs: float32 [384, 16000], P('wa', 'vert')
- chosen: float32 [384], P('wa')
The draws below stay inside these ranges and needn't reach their ends.
Inputs may be any that keep to these rules, and one draw needn't show every extreme that they name: `gate_levels`: whole numbers. `up_levels`: whole numbers. `down_levels`: whole numbers. `gate_scale`: positive. `up_scale`: positive. `down_scale`: positive.
All inputs are finite; a program needn't handle non-finite values.
Results may differ from the reference program's by a relative error of at most 0.0025.
Values may be sent and summed in bfloat16 or wider, within the bound.
A program may use at most 128 MiB of HBM per device.

```python
import math
import jax
import jax.numpy as jnp
import numpy as np
from jax import lax

D = 8192
FF = 28672
RD = 4096
VOCAB = 16000
ROWS = 384
REWARDS = 4


def level_table(key, salt, rows, cols):
    values = jax.random.randint(jax.random.fold_in(key, salt), (rows, cols), -127, 128)
    return values.astype(jnp.float32).astype(jnp.bfloat16)


def scale_table(key, salt, count, unit):
    logs = jax.random.uniform(jax.random.fold_in(key, salt), (count,), jnp.float32, math.log(0.5), math.log(2.0))
    return (jnp.exp(logs) * unit).astype(jnp.float32)


def head_table(key, salt, lead, fan, vocab):
    base_key = jax.random.fold_in(key, salt)
    ramp = 1.0 + 0.7 * jnp.arange(vocab, dtype=jnp.float32) / max(vocab - 1, 1)
    weight = jax.random.normal(jax.random.fold_in(base_key, 1), (lead, fan, vocab), jnp.float32) * (3.0 / math.sqrt(fan)) * ramp
    return weight


def draw_hidden_in(key, part):
    ramp = 1.0 + 2.0 * jnp.arange(D, dtype=jnp.float32) / max(D - 1, 1)
    values = jax.random.normal(jax.random.fold_in(key, 21), (ROWS, D), jnp.float32)
    return (values * ramp).astype(jnp.bfloat16)


def draw_gate_levels(key, part):
    return level_table(key, 31, D, FF)


def draw_up_levels(key, part):
    return level_table(key, 32, D, FF)


def draw_down_levels(key, part):
    return level_table(key, 33, FF, D)


def draw_gate_scale(key, part):
    return scale_table(key, 41, FF, 1.0 / (73.6 * 2.08 * math.sqrt(D)))


def draw_up_scale(key, part):
    return scale_table(key, 42, FF, 1.0 / (73.6 * 2.08 * math.sqrt(D)))


def draw_down_scale(key, part):
    return scale_table(key, 43, D, 1.0 / (73.6 * 0.8 * math.sqrt(FF)))


def draw_head_weight(key, part):
    return head_table(key, 51, 1, D, VOCAB)[0].astype(jnp.bfloat16)


def draw_reward_heads(key, part):
    return head_table(key, 52, REWARDS, RD, VOCAB).astype(jnp.bfloat16)


def place_ends(entries, key, low, largest):
    shape = entries.shape
    index_at = [jax.random.randint(jax.random.fold_in(key, axis), (), 0, shape[axis]) for axis in range(len(shape))]
    entries = entries.at[tuple(index_at)].set(low)
    longest = shape.index(max(shape))
    index_at[longest] = (index_at[longest] + 1) % shape[longest]
    return entries.at[tuple(index_at)].set(largest)


def block_levels(stream_key, shape, split, least, high):
    level, own = 1.0, jax.random.fold_in(stream_key, 6)
    for axis_at, blocks in split:
        steps = jnp.exp(jax.random.uniform(jax.random.fold_in(own, axis_at), (blocks,), jnp.float32, least / len(split), high / len(split)))
        level = level * jnp.repeat(steps, shape[axis_at] // blocks).reshape([-1 if axis == axis_at else 1 for axis in range(len(shape))])
    return level


def cumulative_ranks(amount, skew):
    loads = [(1 << 20) // math.isqrt(standing ** skew) + 1 for standing in range(1, amount + 1)]
    scale = 1 + sum(loads) // (1 << 30)
    return np.cumsum(np.array([max(1, weight // scale) for weight in loads]))


def ranked_ids(rng, shape, amount, lean):
    table = cumulative_ranks(amount, lean)
    pick = jax.random.randint(jax.random.fold_in(rng, 1), shape, 0, int(table[amount - 1]))
    rank = jnp.searchsorted(jnp.asarray(table, jnp.int32), pick, side="right")
    return jax.random.permutation(jax.random.fold_in(rng, 2), amount)[rank].astype(jnp.int32)


def noise(stream_key, shape, spread, limit, cuts=(), kind=jnp.bfloat16):
    drawn = spread * jax.random.normal(stream_key, shape, jnp.float32)
    if cuts:
        drawn = drawn * block_levels(stream_key, shape, cuts, -0.22, 0.18)
    return jnp.clip(drawn, -limit, limit).astype(kind)


def setup_inputs(seed: int = 0) -> dict:
    streams_of = jax.random.split(jax.random.key(seed), 15)
    return {
        "hidden_in": draw_hidden_in(jax.random.fold_in(streams_of[14], 71), 0),
        "gate_levels": draw_gate_levels(jax.random.fold_in(streams_of[14], 71), 0),
        "up_levels": draw_up_levels(jax.random.fold_in(streams_of[14], 71), 0),
        "gate_scale": draw_gate_scale(jax.random.fold_in(streams_of[14], 71), 0),
        "up_scale": draw_up_scale(jax.random.fold_in(streams_of[14], 71), 0),
        "down_levels": draw_down_levels(jax.random.fold_in(streams_of[14], 71), 0),
        "down_scale": draw_down_scale(jax.random.fold_in(streams_of[14], 71), 0),
        "norm_gain": jnp.clip(1.0 + 0.1 * jax.random.normal(streams_of[7], (D,), jnp.float32), 0.5, 1.5),
        "head_weight": draw_head_weight(jax.random.fold_in(streams_of[14], 71), 0),
        "reward_states": noise(streams_of[9], (REWARDS, ROWS, RD), 1.0, 6.0, ((0, 4), (2, 8))),
        "reward_gain": jnp.clip(1.0 + 0.1 * jax.random.normal(streams_of[10], (REWARDS, RD), jnp.float32), 0.5, 1.5),
        "reward_heads": draw_reward_heads(jax.random.fold_in(streams_of[14], 71), 0),
        "preference": place_ends(jax.random.randint(streams_of[12], (ROWS, REWARDS), 0, 17), jax.random.fold_in(streams_of[12], 1), 0, 16).astype(jnp.int32),
        "token_ids": place_ends(ranked_ids(streams_of[13], (ROWS,), VOCAB, 2), jax.random.fold_in(streams_of[13], 3), 0, VOCAB - 1).astype(jnp.int32),
    }


def log_softmax_rows(values):
    top = lax.optimization_barrier(jnp.max(values, axis=1, keepdims=True))
    return values - top - jnp.log(lax.optimization_barrier(jnp.sum(jnp.exp(values - top), axis=1, keepdims=True)))

def reference(hidden_in, gate_levels, up_levels, gate_scale, up_scale, down_levels, down_scale, norm_gain, head_weight, reward_states, reward_gain, reward_heads, preference, token_ids):
    gate = jnp.dot(hidden_in, gate_levels, preferred_element_type=jnp.float32) * gate_scale
    up = jnp.dot(hidden_in, up_levels, preferred_element_type=jnp.float32) * up_scale
    hidden = (jax.nn.silu(gate) * up).astype(jnp.bfloat16)
    down = jnp.dot(hidden, down_levels, preferred_element_type=jnp.float32) * down_scale
    resid = hidden_in.astype(jnp.float32) + down
    normed = (resid * lax.rsqrt(lax.optimization_barrier(jnp.mean(resid * resid, axis=1, keepdims=True)) + 1e-05) * norm_gain).astype(jnp.bfloat16)
    base = jnp.dot(normed, head_weight, preferred_element_type=jnp.float32)
    base_logp = log_softmax_rows(base)
    weights = preference.astype(jnp.float32).T / 16.0

    def one_reward(packed):
        states, gain, head, weight = packed
        values = states.astype(jnp.float32)
        scaled = (values * lax.rsqrt(lax.optimization_barrier(jnp.mean(values * values, axis=1, keepdims=True)) + 1e-05) * gain).astype(jnp.bfloat16)
        logits = jnp.dot(scaled, head, preferred_element_type=jnp.float32)
        return weight[:, None] * log_softmax_rows(logits)
    terms = lax.map(one_reward, (reward_states, reward_gain, reward_heads, weights))
    mix = base_logp + lax.optimization_barrier(jnp.sum(terms, axis=0))
    log_probs = log_softmax_rows(mix)
    chosen = jnp.take_along_axis(log_probs, token_ids.astype(jnp.int32)[:, None], axis=1)[:, 0]
    return (log_probs, chosen)
```

```python
import functools

import jax
import jax.numpy as jnp
from jax import lax
from jax.experimental import pallas as pl
from jax.experimental.pallas import tpu as pltpu
from jax.sharding import PartitionSpec as P

MESH = pl.DeviceIdType.MESH
VMEM = pl.BlockSpec(memory_space=pltpu.VMEM)
ANY = pl.BlockSpec(memory_space=pl.ANY)
LAG = 2
LIMIT = 60 * 2**20


def greet(n, nv):
    i, v = lax.axis_index("wa"), lax.axis_index("vert")
    barrier = pltpu.get_barrier_semaphore()
    for k in range(1, n):
        pl.semaphore_signal(
            barrier, inc=1, device_id={"wa": lax.rem(i + k, n)}, device_id_type=MESH
        )

    def one(k, carry):
        pl.semaphore_signal(
            barrier, inc=1, device_id={"vert": lax.rem(v + k, nv)}, device_id_type=MESH
        )
        return carry

    lax.fori_loop(1, nv, one, 0)
    pl.semaphore_wait(barrier, n - 1 + nv - 1)


def remote(src, dst, send, recv, axis, peer):
    return pltpu.make_async_remote_copy(
        src_ref=src,
        dst_ref=dst,
        send_sem=send,
        recv_sem=recv,
        device_id={axis: peer},
        device_id_type=MESH,
    )


def each(count, body):
    def one(k, carry):
        body(k)
        return carry

    lax.fori_loop(1, count, one, 0)


def mlp_kernel(
    n, nv, chunks, width,
    x_ref, gate_hbm, up_hbm, gate_scale, up_scale, states_ref,
    hid_ref, all_states,
    weights, own, came, going, wsem, rsend, rrecv, hsend, hrecv, ssend, srecv,
):
    i, v = lax.axis_index("wa"), lax.axis_index("vert")
    half = own.shape[2]
    span = states_ref.shape[1]
    greet(n, nv)

    def place(d):
        return all_states.at[:, pl.ds(pl.multiple_of(d * span, span), span)]

    def states_copy(k):
        return remote(
            states_ref, place(v), ssend.at[k], srecv.at[k], "vert", lax.rem(v + k, nv)
        )

    each(nv, lambda k: states_copy(k).start())

    def load(c):
        cols = pl.ds(pl.multiple_of(c * width, width), width)
        slot = lax.rem(c, 2)
        return (
            pltpu.make_async_copy(gate_hbm.at[:, cols], weights.at[slot, 0], wsem.at[slot, 0]),
            pltpu.make_async_copy(up_hbm.at[:, cols], weights.at[slot, 1], wsem.at[slot, 1]),
        )

    for copy in load(0):
        copy.start()
    all_states[:, pl.ds(pl.multiple_of(v * span, span), span)] = states_ref[...]

    def sum_copy(h, c):
        step = 1 if h else -1
        return remote(
            going.at[h, c], came.at[h, c], rsend.at[h, c], rrecv.at[h, c],
            "wa", jnp.clip(i + step, 0, n - 1),
        )

    def hidden_copy(h, c):
        step = -1 if h else 1
        view = hid_ref.at[h, :, pl.ds(pl.multiple_of(c * width, width), width)]
        return remote(
            view, view, hsend.at[h, c], hrecv.at[h, c],
            "wa", jnp.clip(i + step, 0, n - 1),
        )

    def step(s, carry):
        @pl.when(s < chunks)
        def _():
            @pl.when(s + 1 < chunks)
            def _():
                for copy in load(s + 1):
                    copy.start()

            for copy in load(s):
                copy.wait()
            slot = lax.rem(s, 2)
            for m in range(2):
                out = jnp.dot(x_ref[...], weights[slot, m], preferred_element_type=jnp.float32)
                own[s, 0, :, m * width : (m + 1) * width] = out[:half]
                own[s, 1, :, m * width : (m + 1) * width] = out[half:]

        for h in range(2):
            p = i if h else n - 1 - i
            c = s - LAG * p
            here = jnp.logical_and(c >= 0, c < chunks)

            @pl.when(jnp.logical_and(here, p == 0))
            def _():
                going[h, c] = own[c, h].astype(jnp.bfloat16)
                sum_copy(h, c).start()

            @pl.when(jnp.logical_and(here, jnp.logical_and(p > 0, p < n - 1)))
            def _():
                sum_copy(h, c).wait_recv()
                going[h, c] = (own[c, h] + came[h, c].astype(jnp.float32)).astype(jnp.bfloat16)
                sum_copy(h, c).start()

            @pl.when(jnp.logical_and(here, p == n - 1))
            def _():
                sum_copy(h, c).wait_recv()
                total = own[c, h] + came[h, c].astype(jnp.float32)
                gate = total[:, :width] * gate_scale[c]
                up = total[:, width:] * up_scale[c]
                value = (jax.nn.silu(gate) * up).astype(jnp.bfloat16)
                hid_ref[h, :, pl.ds(pl.multiple_of(c * width, width), width)] = value
                hidden_copy(h, c).start()

            q = n - 1 - p
            e = s - LAG * (n - 1) - LAG * q
            there = jnp.logical_and(jnp.logical_and(e >= 0, e < chunks), q > 0)

            @pl.when(there)
            def _():
                hidden_copy(h, e).wait_recv()

            @pl.when(jnp.logical_and(there, q < n - 1))
            def _():
                hidden_copy(h, e).start()

        return carry

    lax.fori_loop(0, chunks + 2 * LAG * (n - 1), step, 0)

    def finish(c, carry):
        for h in range(2):
            p = i if h else n - 1 - i

            @pl.when(p < n - 1)
            def _():
                sum_copy(h, c).wait_send()

            @pl.when(p > 0)
            def _():
                hidden_copy(h, c).wait_send()

        return carry

    lax.fori_loop(0, chunks, finish, 0)

    def states_done(k):
        states_copy(k).wait_send()
        remote(
            states_ref, place(lax.rem(v + nv - k, nv)), ssend.at[k], srecv.at[k],
            "vert", lax.rem(v + k, nv),
        ).wait_recv()

    each(nv, states_done)


def mlp(n, nv, x, gate_levels, up_levels, gate_scale, up_scale, states):
    rows, depth = x.shape
    total = gate_levels.shape[1]
    width = 256 if total % 256 == 0 and total // 256 > 8 else 128
    chunks = total // width
    half = rows // 2
    span = states.shape[1]
    sems = pltpu.SemaphoreType.DMA
    return pl.pallas_call(
        functools.partial(mlp_kernel, n, nv, chunks, width),
        out_shape=(
            jax.ShapeDtypeStruct((2, half, total), jnp.bfloat16),
            jax.ShapeDtypeStruct((rows, span * nv), jnp.bfloat16),
        ),
        in_specs=[VMEM, ANY, ANY, VMEM, VMEM, VMEM],
        out_specs=(VMEM, VMEM),
        scratch_shapes=[
            pltpu.VMEM((2, 2, depth, width), jnp.bfloat16),
            pltpu.VMEM((chunks, 2, half, 2 * width), jnp.float32),
            pltpu.VMEM((2, chunks, half, 2 * width), jnp.bfloat16),
            pltpu.VMEM((2, chunks, half, 2 * width), jnp.bfloat16),
            sems((2, 2)),
            sems((2, chunks)),
            sems((2, chunks)),
            sems((2, chunks)),
            sems((2, chunks)),
            sems((nv,)),
            sems((nv,)),
        ],
        compiler_params=pltpu.CompilerParams(
            collective_id=0, has_side_effects=True, vmem_limit_bytes=LIMIT
        ),
    )(
        x, gate_levels, up_levels,
        gate_scale.reshape(chunks, 1, width), up_scale.reshape(chunks, 1, width), states,
    )


def norm_kernel(
    n, nv, part_ref, x_ref, scale_ref, gain_ref, out_ref,
    came, squares, squares_in, dsend, drecv, qsend, qrecv, nsend, nrecv,
):
    i, v = lax.axis_index("wa"), lax.axis_index("vert")
    greet(n, nv)

    def part_copy(k):
        peer = lax.rem(v + k, nv)
        return remote(part_ref.at[peer], came.at[k], dsend.at[k], drecv.at[k], "vert", peer)

    each(nv, lambda k: part_copy(k).start())
    came[0] = part_ref[v]

    def add(k, acc):
        part_copy(k).wait_recv()
        return acc + came[k].astype(jnp.float32)

    down = lax.fori_loop(1, nv, add, came[0].astype(jnp.float32))
    resid = x_ref[v].astype(jnp.float32) + down * scale_ref[...]
    total = jnp.sum(resid * resid, axis=1, keepdims=True)
    squares[...] = jnp.broadcast_to(total, squares.shape)

    def square_copy(k):
        return remote(
            squares, squares_in.at[k], qsend.at[k], qrecv.at[k], "wa", lax.rem(i + k, n)
        )

    for k in range(1, n):
        square_copy(k).start()
    for k in range(1, n):
        square_copy(k).wait_recv()
        total = total + squares_in[k][:, :1]
    features = resid.shape[1] * n
    out_ref[v] = (resid * lax.rsqrt(total / features + 1e-05) * gain_ref[...]).astype(jnp.bfloat16)

    def norm_copy(k):
        return remote(
            out_ref.at[v], out_ref.at[v], nsend.at[k], nrecv.at[k], "vert", lax.rem(v + k, nv)
        )

    each(nv, lambda k: norm_copy(k).start())

    def done(k):
        other = lax.rem(v + nv - k, nv)
        remote(
            out_ref.at[v], out_ref.at[other], nsend.at[k], nrecv.at[k],
            "vert", lax.rem(v + k, nv),
        ).wait_recv()
        norm_copy(k).wait_send()
        part_copy(k).wait_send()

    each(nv, done)
    for k in range(1, n):
        square_copy(k).wait_send()


def norm(n, nv, part, x, scale, gain):
    rows, depth = x.shape
    block = rows // nv
    sems = pltpu.SemaphoreType.DMA
    out = pl.pallas_call(
        functools.partial(norm_kernel, n, nv),
        out_shape=jax.ShapeDtypeStruct((nv, block, depth), jnp.bfloat16),
        in_specs=[VMEM] * 4,
        out_specs=VMEM,
        scratch_shapes=[
            pltpu.VMEM((nv, block, depth), jnp.bfloat16),
            pltpu.VMEM((block, 128), jnp.float32),
            pltpu.VMEM((n, block, 128), jnp.float32),
            sems((nv,)),
            sems((nv,)),
            sems((n,)),
            sems((n,)),
            sems((nv,)),
            sems((nv,)),
        ],
        compiler_params=pltpu.CompilerParams(
            collective_id=1, has_side_effects=True, vmem_limit_bytes=LIMIT
        ),
    )(part.reshape(nv, block, depth), x.reshape(nv, block, depth), scale[None], gain[None])
    return out.reshape(rows, depth)


def mix_kernel(
    n, nv, part_ref, token_ref, out_ref, chosen_ref,
    came, stats, stats_in, msend, mrecv, tsend, trecv,
):
    i, v = lax.axis_index("wa"), lax.axis_index("vert")
    greet(n, nv)

    def part_copy(k):
        peer = lax.rem(i + k, n)
        return remote(part_ref.at[peer], came.at[k], msend.at[k], mrecv.at[k], "wa", peer)

    for k in range(1, n):
        part_copy(k).start()
    mix = part_ref[i].astype(jnp.float32)
    for k in range(1, n):
        part_copy(k).wait_recv()
        mix = mix + came[k].astype(jnp.float32)
    columns = mix.shape[1]
    top = jnp.max(mix, axis=1, keepdims=True)
    total = jnp.sum(jnp.exp(mix - top), axis=1, keepdims=True)
    index = lax.broadcasted_iota(jnp.int32, mix.shape, 1) + v * columns
    picked = jnp.sum(jnp.where(index == token_ref[...], mix, 0.0), axis=1, keepdims=True)
    out_ref[...] = mix
    lane = lax.broadcasted_iota(jnp.int32, stats.shape, 1)
    stats[...] = jnp.where(lane == 0, top, jnp.where(lane == 1, total, picked))

    def stat_copy(k):
        return remote(
            stats, stats_in.at[k], tsend.at[k], trecv.at[k], "vert", lax.rem(v + k, nv)
        )

    each(nv, lambda k: stat_copy(k).start())

    def merge(k, state):
        top, total, picked = state
        stat_copy(k).wait_recv()
        other = stats_in[k]
        new = jnp.maximum(top, other[:, 0:1])
        total = total * jnp.exp(top - new) + other[:, 1:2] * jnp.exp(other[:, 0:1] - new)
        return new, total, picked + other[:, 2:3]

    top, total, picked = lax.fori_loop(1, nv, merge, (top, total, picked))
    shift = top + jnp.log(total)
    out_ref[...] = out_ref[...] - shift
    chosen_ref[...] = picked - shift
    each(nv, lambda k: stat_copy(k).wait_send())
    for k in range(1, n):
        part_copy(k).wait_send()


def mix_rows(n, nv, part, token_ids):
    rows, columns = part.shape
    block = rows // n
    sems = pltpu.SemaphoreType.DMA
    log_probs, chosen = pl.pallas_call(
        functools.partial(mix_kernel, n, nv),
        out_shape=(
            jax.ShapeDtypeStruct((block, columns), jnp.float32),
            jax.ShapeDtypeStruct((block, 1), jnp.float32),
        ),
        in_specs=[VMEM] * 2,
        out_specs=(VMEM, VMEM),
        scratch_shapes=[
            pltpu.VMEM((n, block, columns), jnp.bfloat16),
            pltpu.VMEM((block, 128), jnp.float32),
            pltpu.VMEM((nv, block, 128), jnp.float32),
            sems((n,)),
            sems((n,)),
            sems((nv,)),
            sems((nv,)),
        ],
        compiler_params=pltpu.CompilerParams(
            collective_id=2, has_side_effects=True, vmem_limit_bytes=LIMIT
        ),
    )(part.reshape(n, block, columns), token_ids[:, None])
    return log_probs, chosen[:, 0]


def local(
    n,
    nv,
    hidden_in,
    gate_levels,
    up_levels,
    gate_scale,
    up_scale,
    down_levels,
    down_scale,
    norm_gain,
    head_weight,
    reward_states,
    reward_gain,
    reward_heads,
    preference,
    token_ids,
):
    rows = hidden_in.shape[0]
    models, _, span = reward_states.shape
    hidden, states = mlp(
        n, nv, hidden_in, gate_levels, up_levels, gate_scale, up_scale,
        jnp.swapaxes(reward_states, 0, 1).reshape(rows, models * span),
    )
    down_part = jnp.dot(
        hidden.reshape(rows, hidden.shape[2]), down_levels, preferred_element_type=jnp.float32
    ).astype(jnp.bfloat16)
    normed = norm(n, nv, down_part, hidden_in, down_scale, norm_gain)
    states = states.reshape(rows, nv, models, span).transpose(2, 0, 1, 3).reshape(models, rows, nv * span)
    state_values = states.astype(jnp.float32)
    state_scale = lax.rsqrt(jnp.mean(state_values * state_values, axis=2, keepdims=True) + 1e-05)
    reward_normed = (state_values * state_scale * reward_gain[:, None, :]).astype(jnp.bfloat16)
    reward_logits = jnp.einsum(
        "rnd,rdv->rnv", reward_normed, reward_heads, preferred_element_type=jnp.float32
    )
    weights = preference.astype(jnp.float32).T / 16.0
    weighted = jnp.sum(weights[:, :, None] * reward_logits, axis=0)
    base_part = jnp.dot(normed, head_weight, preferred_element_type=jnp.float32)
    return mix_rows(n, nv, (base_part + weighted).astype(jnp.bfloat16), token_ids)


def solution(mesh):
    return jax.shard_map(
        functools.partial(local, mesh.shape["wa"], mesh.shape["vert"]),
        mesh=mesh,
        in_specs=(
            P(None, "wa"),
            P("wa", "vert"),
            P("wa", "vert"),
            P("vert"),
            P("vert"),
            P("vert", "wa"),
            P("wa"),
            P("wa"),
            P("wa", "vert"),
            P("wa", None, "vert"),
            P("wa", None),
            P("wa", None, "vert"),
            P(None, "wa"),
            P("wa"),
        ),
        out_specs=(P("wa", "vert"), P("wa")),
        check_vma=False,
    )
```
